512 devices in a mesh: clus: 64 (over z, x, core), nbr: 8 (over y).
Axes of the slice: x: 4, y: 8, z: 8, core: 2. Of those that a mesh axis runs over, the one named last changes fastest.
Arguments:
- panels: bfloat16 [2048, 16, 256], P(('clus', 'nbr')), may hold values from -6 to 6
- leaf_basis: bfloat16 [2048, 256, 64], P(('clus', 'nbr')), may hold values from -0.375 to 0.375
- transfer: bfloat16 [2048, 64, 64], P(('clus', 'nbr')), may hold values from -0.375 to 0.375
- leaf_sources: int32 [2048, 8], P(('clus', 'nbr')), may hold values from 0 to 2047, as said below
- leaf_coupling: bfloat16 [2048, 8, 64, 64], P(('clus', 'nbr')), may hold values from -0.25 to 0.25
- box_sources: int32 [512, 32], P(('clus', 'nbr')), may hold values from 0 to 511
- box_coupling: bfloat16 [512, 32, 64, 64], P(('clus', 'nbr')), may hold values from -0.125 to 0.125
- near_blocks: bfloat16 [8192, 256, 256], P(('clus', 'nbr')), may hold values from -0.125 to 0.125
- near_pairs: int32 [8192, 2], P(('clus', 'nbr')), may hold values from 0 to 2047, as said below
- near_count: int32 [512], P(('clus', 'nbr')), may hold values from 1 to 16, as said below
Outputs:
- first_product: bfloat16 [2048, 16, 256], P(('clus', 'nbr'))
- second_product: bfloat16 [2048, 16, 256], P(('clus', 'nbr'))
The draws below stay inside these ranges and needn't reach their ends.
Inputs may be any that keep to these rules, and one draw needn't show every extreme that they name: `leaf_sources`: each entry names a leaf of the row's own group of 32 consecutive leaves. `near_pairs`: row n is a slot of device n // 16; its first leaf is not above its second, and both lie in that device's group of 32 consecutive leaves. Rows of dead slots hold such pairs too. `near_count`: some device fills all 16 slots in every draw.
All inputs are finite; a program needn't handle non-finite values.
Results may differ from the reference program's by a relative error of at most 0.013.
Values may be sent and summed in bfloat16 or wider, within the bound.
A program may use at most 64 MiB of HBM per device.

```python
import jax
import jax.numpy as jnp
from jax import lax

PANELS = 256
RANK = 64
RHS = 16
LEAF_DEV = 4
NEAR_DEV = 16
FAR_LEAF = 8
FAR_BOX = 32
LEAVES = 2048
BOXES = 512
GROUP = 32
NEAR_TOTAL = 8192
DEVICES = 512


def draw_leaf_sources(key, part):
    picks = jax.random.randint(jax.random.fold_in(key, 31), (LEAVES, FAR_LEAF), 0, GROUP)
    group_base = jnp.arange(LEAVES) // GROUP * GROUP
    return (picks + group_base[:, None]).astype(jnp.int32)


def draw_near_pairs(key, part):
    lower_pick = jax.random.randint(jax.random.fold_in(key, 41), (NEAR_TOTAL,), 0, GROUP)
    upper_pick = jax.random.randint(jax.random.fold_in(key, 42), (NEAR_TOTAL,), 0, GROUP)
    owner_device = jnp.arange(NEAR_TOTAL) // NEAR_DEV
    group_base = owner_device * LEAF_DEV // GROUP * GROUP
    first_leaf = jnp.minimum(lower_pick, upper_pick) + group_base
    second_leaf = jnp.maximum(lower_pick, upper_pick) + group_base
    return jnp.stack([first_leaf, second_leaf], axis=1).astype(jnp.int32)


def draw_near_count(key, part):
    counts = jax.random.randint(jax.random.fold_in(key, 51), (DEVICES,), 1, NEAR_DEV + 1)
    fullest = jax.random.randint(jax.random.fold_in(key, 52), (), 0, DEVICES)
    return counts.at[fullest].set(NEAR_DEV).astype(jnp.int32)


def set_ends(drawn, key, low, largest):
    dims = drawn.shape
    spot = [jax.random.randint(jax.random.fold_in(key, axis), (), 0, dims[axis]) for axis in range(len(dims))]
    drawn = drawn.at[tuple(spot)].set(low)
    longest = dims.index(max(dims))
    spot[longest] = (spot[longest] + 1) % dims[longest]
    return drawn.at[tuple(spot)].set(largest)


def shard_levels(key, shape, split, low, top_value):
    level, own = 1.0, jax.random.fold_in(key, 6)
    for position, shards_of in split:
        draws = jnp.exp(jax.random.uniform(jax.random.fold_in(own, position), (shards_of,), jnp.float32, low / len(split), top_value / len(split)))
        level = level * jnp.repeat(draws, shape[position] // shards_of).reshape([-1 if axis == position else 1 for axis in range(len(shape))])
    return level


def scatter_about(rng, extent, scale, reach, pieces=(), kind=jnp.bfloat16):
    drawn = scale * jax.random.normal(rng, extent, jnp.float32)
    if pieces:
        drawn = drawn * shard_levels(rng, extent, pieces, -0.22, 0.18)
    return jnp.clip(drawn, -reach, reach).astype(kind)


def setup_inputs(seed: int = 0) -> dict:
    keys = jax.random.split(jax.random.key(seed), 11)
    return {
        "panels": scatter_about(keys[0], (LEAVES, RHS, PANELS), 1.0, 6.0, ((0, 512),)),
        "leaf_basis": scatter_about(keys[1], (LEAVES, PANELS, RANK), PANELS ** -0.5, 0.375, ((0, 512),)),
        "transfer": scatter_about(keys[2], (LEAVES, RANK, RANK), (RANK * LEAF_DEV) ** -0.5, 0.375, ((0, 512),)),
        "leaf_sources": draw_leaf_sources(jax.random.fold_in(keys[10], 71), 0),
        "leaf_coupling": scatter_about(keys[4], (LEAVES, FAR_LEAF, RANK, RANK), (RANK * FAR_LEAF) ** -0.5, 0.25, ((0, 512),)),
        "box_sources": set_ends(jax.random.randint(keys[5], (BOXES, FAR_BOX), 0, BOXES), jax.random.fold_in(keys[5], 1), 0, BOXES - 1).astype(jnp.int32),
        "box_coupling": scatter_about(keys[6], (BOXES, FAR_BOX, RANK, RANK), (RANK * FAR_BOX) ** -0.5, 0.125, ((0, 512),)),
        "near_blocks": scatter_about(keys[7], (NEAR_TOTAL, PANELS, PANELS), (2 * PANELS * NEAR_DEV // LEAF_DEV) ** -0.5, 0.125, ((0, 512),)),
        "near_pairs": draw_near_pairs(jax.random.fold_in(keys[10], 71), 0),
        "near_count": draw_near_count(jax.random.fold_in(keys[10], 71), 0),
    }


def product(values, leaf_basis, transfer, leaf_sources, leaf_coupling, box_sources, box_coupling, near_blocks, near_pairs, near_count):
    f32 = jnp.float32
    coefs = jnp.einsum("trp,tpk->trk", values.astype(f32), leaf_basis.astype(f32)).astype(jnp.bfloat16)
    grouped = transfer.astype(f32).reshape(BOXES, LEAF_DEV, RANK, RANK)
    box_coefs = jnp.einsum("btrk,btkm->brm", coefs.astype(f32).reshape(BOXES, LEAF_DEV, RHS, RANK), grouped).astype(jnp.bfloat16)
    box_field = jnp.einsum("bjrk,bjkm->brm", box_coefs[box_sources].astype(f32), box_coupling.astype(f32)).astype(jnp.bfloat16)
    leaf_field = jnp.einsum("tjrk,tjkm->trm", coefs[leaf_sources].astype(f32), leaf_coupling.astype(f32))
    descend = jnp.einsum("brm,btkm->btrk", box_field.astype(f32), grouped).reshape(LEAVES, RHS, RANK)
    leaf_total = (leaf_field + descend).astype(jnp.bfloat16)
    far_part = jnp.einsum("trk,tpk->trp", leaf_total.astype(f32), leaf_basis.astype(f32))
    live_slots = (jnp.arange(NEAR_DEV)[None, :] < near_count[:, None]).astype(f32)
    blocks_dev = near_blocks.reshape(DEVICES, NEAR_DEV, PANELS, PANELS)
    pairs_dev = near_pairs.reshape(DEVICES, NEAR_DEV, 2)

    def one_device(total, item):
        blocks, pairs, live = item
        targets = pairs[:, 0]
        sources = pairs[:, 1]
        from_source = jnp.einsum("nrp,nqp->nrq", values[sources].astype(f32), blocks.astype(f32)) * live[:, None, None]
        apart_mask = live * (targets != sources).astype(f32)
        from_target = jnp.einsum("nrq,nqp->nrp", values[targets].astype(f32), blocks.astype(f32)) * apart_mask[:, None, None]
        total = total.at[targets].add(from_source)
        total = total.at[sources].add(from_target)
        return total, None

    near_part, unused = lax.scan(one_device, jnp.zeros((LEAVES, RHS, PANELS), f32), (blocks_dev, pairs_dev, live_slots))
    return (near_part + far_part).astype(jnp.bfloat16)


def reference(panels, leaf_basis, transfer, leaf_sources, leaf_coupling, box_sources, box_coupling, near_blocks, near_pairs, near_count):
    first_product = product(panels, leaf_basis, transfer, leaf_sources, leaf_coupling, box_sources, box_coupling, near_blocks, near_pairs, near_count)
    second_product = product(first_product, leaf_basis, transfer, leaf_sources, leaf_coupling, box_sources, box_coupling, near_blocks, near_pairs, near_count)
    return (first_product, second_product)
```

```python
import jax
import jax.numpy as jnp
from jax import lax
from jax.experimental import pallas as pl
from jax.experimental.pallas import tpu as pltpu
from jax.sharding import PartitionSpec as P

MESH = pl.DeviceIdType.MESH
F32 = jnp.float32
BF16 = jnp.bfloat16
NY, NZ, NX = 8, 8, 4
LEAVES, RHS, PANELS, RANK = 4, 16, 256, 64
SLOTS, FAR_LEAF, FAR_BOX = 16, 8, 32
GROUP = NY * LEAVES
NT = (((1,), (1,)), ((), ()))
FAR_FIRST = (4, 3, 5, 2, 6, 1, 7)


def dot(a, b):
    return jnp.dot(a, b, preferred_element_type=F32)


def dot_nt(a, b):
    return lax.dot_general(a, b, NT, preferred_element_type=F32)


def iota(shape, dim):
    return lax.broadcasted_iota(jnp.int32, shape, dim)


def kernel(
    pairs, count, leaf_src, box_src,
    panels_hbm, basis_hbm, transfer_hbm, leafc_hbm, boxc_hbm, blocks_hbm,
    out0, out1,
    basis, transfer, leafc, boxw, blocks, twice, leafw, scatter, contrib,
    vals0, vals1, coefs0, coefs1, boxes0, boxes1, part0, part1, got0, got1, boxlhs, leaflhs,
    load_sem, send_sem, recv_sem,
):
    clus = lax.axis_index("clus")
    y = lax.axis_index("nbr")
    core = lax.rem(clus, 2)
    x = lax.rem(clus // 2, NX)
    z = clus // (2 * NX)

    def at(zz, xx, cc, yy):
        return ((zz * NX + xx) * 2 + cc, yy)

    def y_peer(d):
        return at(z, x, core, lax.rem(y + d, NY))

    def z_peer(d):
        return at(lax.rem(z + d, NZ), x, core, y)

    def x_peer(d):
        return at(z, lax.rem(x + d, NX), core, y)

    other = at(z, x, 1 - core, y)

    vals, coefs, boxes = (vals0, vals1), (coefs0, coefs1), (boxes0, boxes1)
    part, got, outs = (part0, part1), (got0, got1), (out0, out1)
    own_rows = pl.ds(y * LEAVES, LEAVES)

    barrier = pltpu.get_barrier_semaphore()
    greet = [y_peer(d) for d in FAR_FIRST] + [z_peer(d) for d in FAR_FIRST]
    greet += [x_peer(d) for d in (2, 1, 3)] + [other]
    for peer in greet:
        pl.semaphore_signal(barrier, inc=1, device_id=peer, device_id_type=MESH)

    loads = [
        pltpu.make_async_copy(panels_hbm, vals0.at[own_rows], load_sem.at[0]),
        pltpu.make_async_copy(basis_hbm, basis, load_sem.at[1]),
        pltpu.make_async_copy(transfer_hbm, transfer, load_sem.at[2]),
        pltpu.make_async_copy(leafc_hbm, leafc, load_sem.at[3]),
        pltpu.make_async_copy(boxc_hbm.at[0], boxw.at[:, pl.ds(0, RANK)], load_sem.at[4]),
        pltpu.make_async_copy(boxc_hbm.at[0], boxw.at[:, pl.ds(RANK, RANK)], load_sem.at[5]),
        pltpu.make_async_copy(blocks_hbm, blocks, load_sem.at[6]),
    ]
    for load in loads:
        load.start()

    lane = iota((1, 2 * RANK), 1)
    low_half = lane < RANK
    eye_row = iota((RANK, 2 * RANK), 0)
    eye_lane = iota((RANK, 2 * RANK), 1)
    loads[2].wait()
    both = (lax.rem(eye_lane, RANK) == eye_row).astype(BF16)
    twice[...] = dot(transfer[...].reshape(LEAVES * RANK, RANK), both).astype(BF16)
    loads[3].wait()
    for t in range(LEAVES):
        place = (eye_lane == eye_row + (t % 2) * RANK).astype(BF16)
        moved = dot(leafc[t].reshape(FAR_LEAF * RANK, RANK), place).astype(BF16)
        moved = moved.reshape(FAR_LEAF, RANK, 2 * RANK)
        leafw[t, :, pl.ds(0, RANK)] = moved
        leafw[t, :, pl.ds(RANK, RANK)] = moved

    slot_of = iota((1, SLOTS * RHS), 1) // RHS
    first = jnp.full((1, SLOTS * RHS), -1, jnp.int32)
    second = jnp.full((1, SLOTS * RHS), -1, jnp.int32)
    live_count = count[0]
    targets = [lax.rem(pairs[0, n], GROUP) for n in range(SLOTS)]
    sources = [lax.rem(pairs[1, n], GROUP) for n in range(SLOTS)]
    for n in range(SLOTS):
        live = n < live_count
        first = jnp.where(slot_of == n, jnp.where(live, targets[n], -1), first)
        apart = jnp.logical_and(live, targets[n] != sources[n])
        second = jnp.where(slot_of == n, jnp.where(apart, sources[n], -1), second)
    rows = NY * LEAVES * RHS
    cols = SLOTS * RHS
    row = iota((rows, cols), 0)
    same = lax.rem(row, RHS) == lax.rem(iota((rows, cols), 1), RHS)
    scatter[:, pl.ds(0, cols)] = jnp.logical_and(same, row // RHS == first).astype(BF16)
    scatter[:, pl.ds(cols, cols)] = jnp.logical_and(same, row // RHS == second).astype(BF16)

    for i in (0, 1, 4, 5, 6):
        loads[i].wait()
    pl.semaphore_wait(barrier, len(greet))

    sent = []

    class Sends:
        def __init__(self, p, base):
            self.p, self.n, self.copies = p, base, []

        def start(self, src, dst, peer):
            copy = pltpu.make_async_remote_copy(
                src_ref=src, dst_ref=dst,
                send_sem=send_sem.at[self.p, self.n], recv_sem=recv_sem.at[self.p, self.n],
                device_id=peer, device_id_type=MESH,
            )
            copy.start()
            self.n += 1
            self.copies.append(copy)
            sent.append(copy)

        def wait(self):
            for copy in self.copies:
                copy.wait_recv()

    diag_row = iota((LEAVES * RHS, LEAVES * RANK), 0) // RHS
    diag_lane = iota((LEAVES * RHS, LEAVES * RANK), 1) // RANK
    diagonal = diag_row == diag_lane

    for p in range(2):
        val, coef, box = vals[p], coefs[p], boxes[p]
        values = Sends(p, 0)
        for d in FAR_FIRST:
            values.start(val.at[own_rows], val.at[own_rows], y_peer(d))

        own = val[own_rows].reshape(LEAVES * RHS, PANELS)
        every = dot_nt(own, basis[...].reshape(LEAVES * RANK, PANELS))
        every = jnp.where(diagonal, every, 0.0).reshape(LEAVES, RHS, LEAVES * RANK)
        packed = jnp.sum(every, axis=0).astype(BF16)
        coef[y, 0] = packed[:, : 2 * RANK]
        coef[y, 1] = packed[:, 2 * RANK :]
        wide = dot(packed, twice[...])
        box[core, x, z, y] = jnp.where(low_half, wide[:8], wide[8:]).astype(BF16)
        along_y = Sends(p, 7)
        mine = box.at[core, x, z, y]
        for d in FAR_FIRST:
            along_y.start(mine, mine, y_peer(d))
        near_coefs = Sends(p, 14)
        for d in FAR_FIRST:
            near_coefs.start(coef.at[y], coef.at[y], y_peer(d))

        along_y.wait()
        along_z = Sends(p, 21)
        mine = box.at[core, x, z]
        for d in FAR_FIRST:
            along_z.start(mine, mine, z_peer(d))

        values.wait()
        for n in range(SLOTS):
            block = blocks[n]
            contrib[pl.ds(n * RHS, RHS)] = dot_nt(val[sources[n]], block).astype(BF16)
            contrib[pl.ds(cols + n * RHS, RHS)] = dot(val[targets[n]], block).astype(BF16)
        total = dot(scatter[...], contrib[...]).astype(BF16)
        part[p][...] = total.reshape(NY, LEAVES * RHS, PANELS)
        near = Sends(p, 28)
        for d in FAR_FIRST:
            near.start(part[p].at[lax.rem(y + d, NY)], got[p].at[d - 1], y_peer(d))

        along_z.wait()
        along_x = Sends(p, 35)
        mine = box.at[core, x]
        for d in (2, 1, 3):
            along_x.start(mine, mine, x_peer(d))
        across = Sends(p, 38)
        across.start(mine, mine, other)

        near_coefs.wait()
        for t in range(LEAVES):
            for j in range(FAR_LEAF):
                leaf = lax.rem(leaf_src[t, j], GROUP)
                tile = coef[lax.div(leaf, LEAVES), lax.div(lax.rem(leaf, LEAVES), 2)]
                keep = (lane // RANK) == lax.rem(leaf, 2)
                leaflhs[t, :, pl.ds(j * 2 * RANK, 2 * RANK)] = jnp.where(
                    keep, tile.astype(F32), 0.0
                ).astype(BF16)
        pair = FAR_LEAF * 2 * RANK
        fields = []
        for t in range(LEAVES):
            fields.append(dot(leaflhs[t], leafw[t].reshape(pair, 2 * RANK)))
        leaf_field = jnp.concatenate([fields[0] + fields[1], fields[2] + fields[3]], axis=1)

        for copy, d in zip(along_x.copies, (2, 1, 3)):
            copy.wait_recv()
            arrived = box.at[core, lax.rem(x + NX - d, NX)]
            across.start(arrived, arrived, other)
        across.wait()

        for j in range(FAR_BOX):
            b = box_src[0, j]
            by = lax.rem(b, NY)
            bc = lax.rem(lax.div(b, NY), 2)
            bx = lax.rem(lax.div(b, 2 * NY), NX)
            bz = lax.div(b, 2 * NY * NX)
            tile = box[bc, bx, bz, by].astype(F32)
            boxlhs[:, pl.ds(j * 2 * RANK, 2 * RANK)] = jnp.concatenate(
                [jnp.where(low_half, tile, 0.0), jnp.where(low_half, 0.0, tile)], axis=0
            ).astype(BF16)
        box_field = dot(boxlhs[...], boxw[...].reshape(FAR_BOX * 2 * RANK, RANK)).astype(BF16)
        descend = dot_nt(box_field, transfer[...].reshape(LEAVES * RANK, RANK))
        leaf_total = leaf_field + descend
        spread = jnp.where(diagonal, jnp.concatenate([leaf_total] * LEAVES, axis=0), 0.0)
        result = dot(spread.astype(BF16), basis[...].reshape(LEAVES * RANK, PANELS))

        near.wait()
        result = result + part[p][y].astype(F32)
        for d in range(1, NY):
            result = result + got[p][d - 1].astype(F32)
        result = result.astype(BF16).reshape(LEAVES, RHS, PANELS)
        outs[p][...] = result
        if p == 0:
            vals1[own_rows] = result

    for copy in sent:
        copy.wait_send()


def on_device(
    panels, leaf_basis, transfer, leaf_sources, leaf_coupling,
    box_sources, box_coupling, near_blocks, near_pairs, near_count,
):
    smem = pl.BlockSpec(memory_space=pltpu.SMEM)
    hbm = pl.BlockSpec(memory_space=pl.ANY)
    vmem = pl.BlockSpec(memory_space=pltpu.VMEM)
    product = jax.ShapeDtypeStruct((LEAVES, RHS, PANELS), BF16)
    values = pltpu.VMEM((NY * LEAVES, RHS, PANELS), BF16)
    coefs = pltpu.VMEM((NY, 2, RHS, 2 * RANK), BF16)
    boxes = pltpu.VMEM((2, NX, NZ, NY, 8, 2 * RANK), BF16)
    part = pltpu.VMEM((NY, LEAVES * RHS, PANELS), BF16)
    got = pltpu.VMEM((NY - 1, LEAVES * RHS, PANELS), BF16)
    copies = 42
    return pl.pallas_call(
        kernel,
        out_shape=(product, product),
        in_specs=[smem] * 4 + [hbm] * 6,
        out_specs=(vmem, vmem),
        scratch_shapes=[
            pltpu.VMEM((LEAVES, RANK, PANELS), BF16),
            pltpu.VMEM((LEAVES, RANK, RANK), BF16),
            pltpu.VMEM((LEAVES, FAR_LEAF, RANK, RANK), BF16),
            pltpu.VMEM((FAR_BOX, 2 * RANK, RANK), BF16),
            pltpu.VMEM((SLOTS, PANELS, PANELS), BF16),
            pltpu.VMEM((LEAVES * RANK, 2 * RANK), BF16),
            pltpu.VMEM((LEAVES, FAR_LEAF, 2 * RANK, 2 * RANK), BF16),
            pltpu.VMEM((NY * LEAVES * RHS, 2 * SLOTS * RHS), BF16),
            pltpu.VMEM((2 * SLOTS * RHS, PANELS), BF16),
            values, values, coefs, coefs, boxes, boxes, part, part, got, got,
            pltpu.VMEM((RHS, FAR_BOX * 2 * RANK), BF16),
            pltpu.VMEM((LEAVES, RHS, FAR_LEAF * 2 * RANK), BF16),
            pltpu.SemaphoreType.DMA((7,)),
            pltpu.SemaphoreType.DMA((2, copies)),
            pltpu.SemaphoreType.DMA((2, copies)),
        ],
        compiler_params=pltpu.CompilerParams(
            collective_id=0, has_side_effects=True, vmem_limit_bytes=40 << 20
        ),
        name="two_products",
    )(
        near_pairs.T, near_count, leaf_sources, box_sources,
        panels, jnp.swapaxes(leaf_basis, 1, 2), transfer, leaf_coupling,
        box_coupling, near_blocks,
    )


def solution(mesh):
    split = ("clus", "nbr")
    placed = (
        P(split, None, None),
        P(split, None, None),
        P(split, None, None),
        P(split, None),
        P(split, None, None, None),
        P(split, None),
        P(split, None, None, None),
        P(split, None, None),
        P(split, None),
        P(split),
    )
    return jax.shard_map(
        on_device,
        mesh=mesh,
        in_specs=placed,
        out_specs=(P(split, None, None), P(split, None, None)),
        check_vma=False,
    )
```

```python
import jax
import jax.numpy as jnp
from jax import lax
from jax.experimental import pallas as pl
from jax.experimental.pallas import tpu as pltpu
from jax.sharding import PartitionSpec as P

MESH = pl.DeviceIdType.MESH
F32 = jnp.float32
BF16 = jnp.bfloat16
NY, NZ, NX = 8, 8, 4
LEAVES, RHS, PANELS, RANK = 4, 16, 256, 64
HALF = RHS // 2
WIDE = LEAVES * RANK
SLOTS, FAR_LEAF, FAR_BOX = 16, 8, 32
GROUP = NY * LEAVES
NT = (((1,), (1,)), ((), ()))
FAR_FIRST = (4, 3, 5, 2, 6, 1, 7)
ORDER = {0: 0, 1: 1, 7: 2, 2: 3, 6: 4, 3: 5, 5: 6, 4: 7}
NEAR, ALL = 5, 8


def dot(a, b):
    return jnp.dot(a, b, preferred_element_type=F32)


def dot_nt(a, b):
    return lax.dot_general(a, b, NT, preferred_element_type=F32)


def iota(shape, dim):
    return lax.broadcasted_iota(jnp.int32, shape, dim)


def ring_slot(distance):
    return jnp.where(distance > 4, 2 * (8 - distance), jnp.maximum(2 * distance - 1, 0))


def kernel(
    pairs, count, leaf_src, box_src, box_src_hbm,
    panels_hbm, basis_hbm, transfer_hbm, leafc_hbm, boxc_hbm, blocks_hbm,
    out_hbm,
    basis, transfer, leafc, boxw, blocks, twice, leafw, scatter, contrib,
    vals00, vals01, vals10, vals11, coefs0, coefs1, boxes0, boxes1, part0, part1, got0, got1,
    last, boxlhs, leaflhs, give0, give1, take0, take1, other_src, other_src_smem,
    load_sem, store_sem, send_sem, recv_sem,
):
    clus = lax.axis_index("clus")
    y = lax.axis_index("nbr")
    core = lax.rem(clus, 2)
    x = lax.rem(lax.div(clus, 2), NX)
    z = lax.div(clus, 2 * NX)

    def at(zz, xx, cc, yy):
        return ((zz * NX + xx) * 2 + cc, yy)

    def y_peer(d):
        return at(z, x, core, lax.rem(y + d, NY))

    def z_peer(d):
        return at(lax.rem(z + d, NZ), x, core, y)

    def x_peer(d):
        return at(z, lax.rem(x + d, NX), core, y)

    other = at(z, x, 1 - core, y)
    own = pl.ds(y * LEAVES, LEAVES)

    barrier = pltpu.get_barrier_semaphore()
    greet = [y_peer(d) for d in FAR_FIRST] + [z_peer(d) for d in FAR_FIRST]
    greet += [x_peer(d) for d in (2, 1, 3)] + [other]
    for peer in greet:
        pl.semaphore_signal(barrier, inc=1, device_id=peer, device_id_type=MESH)

    def load(i, src, dst):
        copy = pltpu.make_async_copy(src, dst, load_sem.at[i])
        copy.start()
        return copy

    loads = [
        load(0, panels_hbm.at[:, pl.ds(0, HALF)], vals00.at[own]),
        load(1, panels_hbm.at[:, pl.ds(HALF, HALF)], vals01.at[own]),
        load(2, basis_hbm, basis),
        load(3, transfer_hbm, transfer),
        load(4, leafc_hbm, leafc),
        load(5, boxc_hbm.at[0], boxw.at[0, :, pl.ds(0, RANK)]),
        load(6, boxc_hbm.at[0], boxw.at[0, :, pl.ds(RANK, RANK)]),
        load(7, blocks_hbm, blocks),
    ]

    lane = iota((1, 2 * RANK), 1)
    low_half = lane < RANK
    eye_row = iota((RANK, 2 * RANK), 0)
    eye_lane = iota((RANK, 2 * RANK), 1)
    diag_row = jnp.bitwise_and(lax.shift_right_logical(iota((LEAVES * RHS, WIDE), 0), 3), LEAVES - 1)
    diagonal = diag_row == lax.shift_right_logical(iota((LEAVES * RHS, WIDE), 1), 6)

    loads[3].wait()
    both = (jnp.bitwise_and(eye_lane, RANK - 1) == eye_row).astype(BF16)
    twice[...] = dot(transfer[...].reshape(WIDE, RANK), both).astype(BF16)

    def upward(val, coef, box):
        mine = jnp.concatenate(
            [val[h][own].reshape(LEAVES * HALF, PANELS) for h in range(2)], axis=0
        )
        every = dot_nt(mine, basis[...].reshape(WIDE, PANELS))
        every = jnp.where(diagonal, every, 0.0).reshape(2, LEAVES, HALF, WIDE)
        packed = jnp.sum(every, axis=1).reshape(RHS, WIDE).astype(BF16)
        coef[y, 0] = packed[:, : 2 * RANK]
        coef[y, 1] = packed[:, 2 * RANK :]
        wide = dot(packed, twice[...])
        box[0, 0] = jnp.where(low_half, wide[:HALF], wide[HALF:]).astype(BF16)

    targets = [lax.rem(pairs[0, n], GROUP) for n in range(SLOTS)]
    sources = [lax.rem(pairs[1, n], GROUP) for n in range(SLOTS)]

    def prepare():
        side = iota((1, 2 * SLOTS * HALF), 1)
        slot = lax.shift_right_logical(side, 3)
        onto = jnp.full(side.shape, -1, jnp.int32)
        live_count = count[0]
        for n in range(SLOTS):
            live = n < live_count
            onto = jnp.where(slot == n, jnp.where(live, targets[n], -1), onto)
            apart = jnp.logical_and(live, targets[n] != sources[n])
            onto = jnp.where(slot == n + SLOTS, jnp.where(apart, sources[n], -1), onto)
        square = (GROUP * HALF, 2 * SLOTS * HALF)
        row = iota(square, 0)
        same = jnp.bitwise_and(row, HALF - 1) == jnp.bitwise_and(iota(square, 1), HALF - 1)
        hit = jnp.logical_and(same, lax.shift_right_logical(row, 3) == onto)
        scatter[...] = hit.astype(BF16)
        loads[4].wait()
        for t in range(LEAVES):
            place = (eye_lane == eye_row + (t % 2) * RANK).astype(BF16)
            moved = dot(leafc[t].reshape(FAR_LEAF * RANK, RANK), place).astype(BF16)
            moved = moved.reshape(FAR_LEAF, RANK, 2 * RANK)
            leafw[t, :, pl.ds(0, RANK)] = moved
            leafw[t, :, pl.ds(RANK, RANK)] = moved

    for i in (0, 1, 2):
        loads[i].wait()
    upward((vals00, vals01), coefs0, boxes0)
    pl.semaphore_wait(barrier, len(greet))

    pending = []

    class Sends:
        def __init__(self, p, k, whole):
            self.p, self.k = p, k
            pending.append((whole, send_sem.at[p, k]))

        def start(self, src, dst, peer, arrival=None):
            pltpu.make_async_remote_copy(
                src_ref=src, dst_ref=dst,
                send_sem=send_sem.at[self.p, self.k],
                recv_sem=recv_sem.at[self.p, self.k if arrival is None else arrival],
                device_id=peer, device_id_type=MESH,
            ).start()

    def finish(p, k, whole):
        pltpu.make_async_copy(whole, whole, recv_sem.at[p, k]).wait()

    V0, V1, C, YN, YF, ZN, ZF, X0, X1, K, R0, R1, W, S = range(14)

    for p in range(2):
        val, coef, box = (
            ((vals00, vals01), coefs0, boxes0),
            ((vals10, vals11), coefs1, boxes1),
        )[p]
        part, got = ((part0, got0), (part1, got1))[p]
        give, take = ((give0, take0), (give1, take1))[p]

        def send_values(h):
            group = Sends(p, (V0, V1)[h], val[h].at[pl.ds(0, 7 * LEAVES)])
            for d in FAR_FIRST:
                group.start(val[h].at[own], val[h].at[own], y_peer(d))

        def near_half(h):
            finish(p, (V0, V1)[h], val[h].at[pl.ds(0, 7 * LEAVES)])
            for n in range(0, SLOTS, 2):
                ahead = [dot_nt(val[h][sources[n + i]], blocks[n + i]) for i in range(2)]
                back = [dot(val[h][targets[n + i]], blocks[n + i]) for i in range(2)]
                contrib[h, pl.ds(n * HALF, RHS)] = jnp.concatenate(ahead, 0).astype(BF16)
                contrib[h, pl.ds((SLOTS + n) * HALF, RHS)] = jnp.concatenate(back, 0).astype(BF16)
            total = dot(scatter[...], contrib[h]).astype(BF16)
            part[h] = total.reshape(NY, LEAVES * HALF, PANELS)
            group = Sends(p, (R0, R1)[h], got.at[h])
            for d in FAR_FIRST:
                group.start(part.at[h, lax.rem(y + d, NY)], got.at[h, d - 1], y_peer(d))

        if p == 1:
            upward(val, coef, box)
        group = Sends(p, YN, box.at[0, pl.ds(1, 7)])
        for d in FAR_FIRST:
            slot = ORDER[8 - d]
            group.start(box.at[0, 0], box.at[0, slot], y_peer(d), YN if slot < NEAR else YF)
        send_values(0)
        send_values(1)
        if p == 0:
            Sends(0, S, other_src).start(box_src_hbm, other_src, other)
        group = Sends(p, C, coef.at[pl.ds(0, 7)])
        for d in FAR_FIRST:
            group.start(coef.at[y], coef.at[y], y_peer(d))

        if p == 0:
            prepare()
            for i in (5, 6, 7):
                loads[i].wait()
            Sends(0, W, boxw.at[1]).start(boxw.at[0], boxw.at[1], other)
            finish(0, S, other_src)
            to_smem = pltpu.make_async_copy(other_src, other_src_smem, load_sem.at[8])
            to_smem.start()
            to_smem.wait()

        for k, a, b in ((YN, 0, NEAR), (YF, NEAR, ALL)):
            finish(p, k, box.at[0, pl.ds(max(a, 1), b - max(a, 1))])
            group = Sends(p, (ZN, ZF)[a > 0], box.at[0, pl.ds(0, 7 * (b - a))])
            for d in FAR_FIRST:
                slot = ORDER[8 - d]
                group.start(
                    box.at[0, pl.ds(a, b - a)], box.at[0, pl.ds(8 * slot + a, b - a)],
                    z_peer(d), ZN if slot < NEAR else ZF,
                )

        def send_x(a, b, k):
            group = Sends(p, k, box.at[pl.ds(1, 3), pl.ds(8 * a, 8 * (b - a))])
            rows = pl.ds(8 * a, 8 * (b - a))
            for d in (2, 1, 3):
                group.start(box.at[0, rows], box.at[NX - d, rows], x_peer(d))

        near_half(0)
        finish(p, ZN, box.at[0, pl.ds(8, 8 * (NEAR - 1))])
        send_x(0, NEAR, X0)
        near_half(1)
        finish(p, ZF, box.at[0, pl.ds(8 * NEAR, 8 * (ALL - NEAR))])
        send_x(NEAR, ALL, X1)

        finish(p, C, coef.at[pl.ds(0, 7)])
        for t in range(LEAVES):
            for j in range(FAR_LEAF):
                leaf = lax.rem(leaf_src[t, j], GROUP)
                tile = coef[lax.div(leaf, LEAVES), lax.div(lax.rem(leaf, LEAVES), 2)]
                keep = lax.shift_right_logical(lane, 6) == lax.rem(leaf, 2)
                leaflhs[t, :, pl.ds(j * 2 * RANK, 2 * RANK)] = jnp.where(
                    keep, tile.astype(F32), 0.0
                ).astype(BF16)
        pair = FAR_LEAF * 2 * RANK
        fields = []
        for t in range(LEAVES):
            fields.append(dot(leaflhs[t], leafw[t].reshape(pair, 2 * RANK)))
        leaf_field = jnp.concatenate([fields[0] + fields[1], fields[2] + fields[3]], axis=1)

        for a, b, k in ((0, NEAR, X0), (NEAR, ALL, X1)):
            finish(p, k, box.at[pl.ds(1, 3), pl.ds(8 * a, 8 * (b - a))])
        if p == 0:
            finish(0, W, boxw.at[1])

        def box_part(g):
            src = (box_src, other_src_smem)[g]
            for j in range(FAR_BOX):
                b = src[0, j]
                by = lax.rem(lax.rem(b, NY) + NY - y, NY)
                held = lax.rem(lax.div(b, NY), 2) == core
                bx = lax.rem(lax.rem(lax.div(b, 2 * NY), NX) + NX - x, NX)
                bz = lax.rem(lax.rem(lax.div(b, 2 * NY * NX), NZ) + NZ - z, NZ)
                tile = box[bx, ring_slot(bz) * NY + ring_slot(by)].astype(F32)
                tile = jnp.where(held, tile, 0.0)
                boxlhs[g, :, pl.ds(j * 2 * RANK, 2 * RANK)] = jnp.concatenate(
                    [jnp.where(low_half, tile, 0.0), jnp.where(low_half, 0.0, tile)], axis=0
                ).astype(BF16)
            return dot(boxlhs[g], boxw[g].reshape(FAR_BOX * 2 * RANK, RANK))

        give[...] = box_part(1)
        Sends(p, K, take).start(give, take, other)
        box_field = box_part(0)
        finish(p, K, take)
        box_field = (box_field + take[...]).astype(BF16)
        descend = dot_nt(box_field, transfer[...].reshape(WIDE, RANK))
        leaf_total = leaf_field + descend
        spread = jnp.concatenate(
            [leaf_total[:HALF]] * LEAVES + [leaf_total[HALF:]] * LEAVES, axis=0
        )
        spread = jnp.where(diagonal, spread, 0.0).astype(BF16)
        far = dot(spread, basis[...].reshape(WIDE, PANELS))

        result = []
        for h in range(2):
            finish(p, (R0, R1)[h], got.at[h])
            near = part[h, y].astype(F32)
            for d in range(1, NY):
                near = near + got[h, d - 1].astype(F32)
            near = near + far[h * LEAVES * HALF : (h + 1) * LEAVES * HALF]
            near = near.astype(BF16).reshape(LEAVES, HALF, PANELS)
            if p == 0:
                (vals10, vals11)[h][own] = near
            else:
                last[h] = near
        for h in range(2):
            pltpu.make_async_copy(
                (vals10, vals11)[h].at[own] if p == 0 else last.at[h],
                out_hbm.at[p, :, pl.ds(h * HALF, HALF)],
                store_sem.at[p, h],
            ).start()

    for whole, sem in pending:
        pltpu.make_async_copy(whole, whole, sem).wait()
    for p in range(2):
        for h in range(2):
            pltpu.make_async_copy(
                (vals10, vals11)[h].at[own] if p == 0 else last.at[h],
                out_hbm.at[p, :, pl.ds(h * HALF, HALF)],
                store_sem.at[p, h],
            ).wait()


def on_device(
    panels, leaf_basis, transfer, leaf_sources, leaf_coupling,
    box_sources, box_coupling, near_blocks, near_pairs, near_count,
):
    smem = pl.BlockSpec(memory_space=pltpu.SMEM)
    hbm = pl.BlockSpec(memory_space=pl.ANY)
    products = jax.ShapeDtypeStruct((2, LEAVES, RHS, PANELS), BF16)
    values = pltpu.VMEM((GROUP, HALF, PANELS), BF16)
    coefs = pltpu.VMEM((NY, 2, RHS, 2 * RANK), BF16)
    boxes = pltpu.VMEM((NX, NZ * NY, HALF, 2 * RANK), BF16)
    part = pltpu.VMEM((2, NY, LEAVES * HALF, PANELS), BF16)
    got = pltpu.VMEM((2, NY - 1, LEAVES * HALF, PANELS), BF16)
    field = pltpu.VMEM((RHS, RANK), F32)
    both = pl.pallas_call(
        kernel,
        out_shape=products,
        in_specs=[smem] * 4 + [hbm] * 7,
        out_specs=hbm,
        scratch_shapes=[
            pltpu.VMEM((LEAVES, RANK, PANELS), BF16),
            pltpu.VMEM((LEAVES, RANK, RANK), BF16),
            pltpu.VMEM((LEAVES, FAR_LEAF, RANK, RANK), BF16),
            pltpu.VMEM((2, FAR_BOX, 2 * RANK, RANK), BF16),
            pltpu.VMEM((SLOTS, PANELS, PANELS), BF16),
            pltpu.VMEM((WIDE, 2 * RANK), BF16),
            pltpu.VMEM((LEAVES, FAR_LEAF, 2 * RANK, 2 * RANK), BF16),
            pltpu.VMEM((GROUP * HALF, 2 * SLOTS * HALF), BF16),
            pltpu.VMEM((2, 2 * SLOTS * HALF, PANELS), BF16),
            values, values, values, values, coefs, coefs, boxes, boxes, part, part, got, got,
            pltpu.VMEM((2, LEAVES, HALF, PANELS), BF16),
            pltpu.VMEM((2, RHS, FAR_BOX * 2 * RANK), BF16),
            pltpu.VMEM((LEAVES, RHS, FAR_LEAF * 2 * RANK), BF16),
            field, field, field, field,
            pltpu.VMEM((1, FAR_BOX), jnp.int32),
            pltpu.SMEM((1, FAR_BOX), jnp.int32),
            pltpu.SemaphoreType.DMA((9,)),
            pltpu.SemaphoreType.DMA((2, 2)),
            pltpu.SemaphoreType.DMA((2, 14)),
            pltpu.SemaphoreType.DMA((2, 14)),
        ],
        compiler_params=pltpu.CompilerParams(
            collective_id=0, has_side_effects=True, vmem_limit_bytes=63 << 20
        ),
        name="two_products",
    )(
        near_pairs.T, near_count, leaf_sources, box_sources, box_sources,
        panels, jnp.swapaxes(leaf_basis, 1, 2), transfer, leaf_coupling,
        box_coupling, near_blocks,
    )
    return both[0], both[1]


def solution(mesh):
    split = ("clus", "nbr")
    placed = (
        P(split, None, None),
        P(split, None, None),
        P(split, None, None),
        P(split, None),
        P(split, None, None, None),
        P(split, None),
        P(split, None, None, None),
        P(split, None, None),
        P(split, None),
        P(split),
    )
    return jax.shard_map(
        on_device,
        mesh=mesh,
        in_specs=placed,
        out_specs=(P(split, None, None), P(split, None, None)),
        check_vma=False,
    )
```

```python
import jax
import jax.numpy as jnp
from jax import lax
from jax.experimental import pallas as pl
from jax.experimental.pallas import tpu as pltpu
from jax.sharding import PartitionSpec as P

MESH = pl.DeviceIdType.MESH
F32 = jnp.float32
BF16 = jnp.bfloat16
NY, NZ, NX = 8, 8, 4
LEAVES, RHS, PANELS, RANK = 4, 16, 256, 64
HALF = RHS // 2
WIDE = LEAVES * RANK
SLOTS, FAR_LEAF, FAR_BOX = 16, 8, 32
GROUP = NY * LEAVES
PLANE = NZ * NY
BOXES = NX * PLANE
NT = (((1,), (1,)), ((), ()))
FAR_FIRST = (4, 3, 5, 2, 6, 1, 7)
NEAR_FIRST = FAR_FIRST[::-1]
ORDER = {0: 0, 1: 1, 7: 2, 2: 3, 6: 4, 3: 5, 5: 6, 4: 7}
NEAR, ALL = 5, 8


def dot(a, b):
    return jnp.dot(a, b, preferred_element_type=F32)


def dot_nt(a, b):
    return lax.dot_general(a, b, NT, preferred_element_type=F32)


def iota(shape, dim):
    return lax.broadcasted_iota(jnp.int32, shape, dim)


def ring_slot(distance):
    return jnp.where(distance > 4, 2 * (8 - distance), jnp.maximum(2 * distance - 1, 0))


def kernel(
    pairs_hbm, count_hbm, leaf_src_hbm, box_src_hbm,
    panels_hbm, basis_hbm, transfer_hbm, leafc_hbm, boxc_hbm, blocks_hbm,
    out_hbm,
    basis, transfer, leafc, boxw, blocks, twice, leafw, scatter, contrib,
    vals00, vals01, vals10, vals11, coefs0, coefs1, boxes0, boxes1, part0, part1, got0, got1,
    last, boxlhs, leaflhs, give0, give1, take0, take1, other_src, other_src_smem,
    pairs, count, leaf_src, box_src, where, down, load_sem, store_sem, send_sem, recv_sem,
):
    clus = lax.axis_index("clus")
    y = lax.axis_index("nbr")
    core = lax.rem(clus, 2)
    x = lax.rem(lax.div(clus, 2), NX)
    z = lax.div(clus, 2 * NX)

    def at(zz, xx, cc, yy):
        return ((zz * NX + xx) * 2 + cc, yy)

    def y_peer(d):
        return at(z, x, core, lax.rem(y + d, NY))

    def z_peer(d):
        return at(lax.rem(z + d, NZ), x, core, y)

    def x_peer(d):
        return at(z, lax.rem(x + d, NX), core, y)

    other = at(z, x, 1 - core, y)
    own = pl.ds(y * LEAVES, LEAVES)

    def load(i, src, dst):
        copy = pltpu.make_async_copy(src, dst, load_sem.at[i])
        copy.start()
        return copy

    loads = [
        load(0, panels_hbm.at[:, pl.ds(0, HALF)], vals00.at[own]),
        load(1, panels_hbm.at[:, pl.ds(HALF, HALF)], vals01.at[own]),
        load(2, basis_hbm, basis),
        load(3, transfer_hbm, transfer),
        load(4, leafc_hbm, leafc),
        load(5, boxc_hbm.at[0], boxw.at[0, :, pl.ds(0, RANK)]),
        load(6, boxc_hbm.at[0], boxw.at[0, :, pl.ds(RANK, RANK)]),
        load(7, blocks_hbm, blocks),
        load(9, pairs_hbm, pairs),
        load(10, count_hbm, count),
        load(11, leaf_src_hbm, leaf_src),
        load(12, box_src_hbm, box_src),
    ]

    barrier = pltpu.get_barrier_semaphore()
    greet = [y_peer(d) for d in FAR_FIRST] + [z_peer(d) for d in FAR_FIRST]
    greet += [x_peer(d) for d in (2, 1, 3)] + [other]
    for peer in greet:
        pl.semaphore_signal(barrier, inc=1, device_id=peer, device_id_type=MESH)

    lane = iota((1, 2 * RANK), 1)
    low_half = lane < RANK
    eye_row = iota((RANK, 2 * RANK), 0)
    eye_lane = iota((RANK, 2 * RANK), 1)
    diag_row = jnp.bitwise_and(lax.shift_right_logical(iota((LEAVES * RHS, WIDE), 0), 3), LEAVES - 1)
    diagonal = diag_row == lax.shift_right_logical(iota((LEAVES * RHS, WIDE), 1), 6)

    loads[3].wait()
    both = (jnp.bitwise_and(eye_lane, RANK - 1) == eye_row).astype(BF16)
    twice[...] = dot(transfer[...].reshape(WIDE, RANK), both).astype(BF16)

    def upward(val, coef, box):
        mine = jnp.concatenate(
            [val[h][own].reshape(LEAVES * HALF, PANELS) for h in range(2)], axis=0
        )
        every = dot_nt(mine, basis[...].reshape(WIDE, PANELS))
        every = jnp.where(diagonal, every, 0.0).reshape(2, LEAVES, HALF, WIDE)
        packed = jnp.sum(every, axis=1).reshape(RHS, WIDE).astype(BF16)
        coef[y, 0] = packed[:, : 2 * RANK]
        coef[y, 1] = packed[:, 2 * RANK :]
        wide = dot(packed, twice[...])
        box[0] = jnp.where(low_half, wide[:HALF], wide[HALF:]).astype(BF16)
        box[BOXES] = jnp.zeros((HALF, 2 * RANK), BF16)

    def prepare():
        side = iota((1, 2 * SLOTS * HALF), 1)
        slot = lax.shift_right_logical(side, 3)
        onto = jnp.full(side.shape, -1, jnp.int32)
        live_count = count[0]
        for n in range(SLOTS):
            live = n < live_count
            onto = jnp.where(slot == n, jnp.where(live, targets[n], -1), onto)
            apart = jnp.logical_and(live, targets[n] != sources[n])
            onto = jnp.where(slot == n + SLOTS, jnp.where(apart, sources[n], -1), onto)
        square = (GROUP * HALF, 2 * SLOTS * HALF)
        row = iota(square, 0)
        same = jnp.bitwise_and(row, HALF - 1) == jnp.bitwise_and(iota(square, 1), HALF - 1)
        hit = jnp.logical_and(same, lax.shift_right_logical(row, 3) == onto)
        scatter[...] = hit.astype(BF16)
        for t in range(LEAVES):
            down[:, pl.ds(t * PANELS, PANELS)] = lax.dot_general(
                transfer[t], basis[t], (((0,), (0,)), ((), ())), preferred_element_type=F32
            ).astype(BF16)
        loads[4].wait()
        for t in range(LEAVES):
            place = (eye_lane == eye_row + (t % 2) * RANK).astype(BF16)
            moved = dot(leafc[t].reshape(FAR_LEAF * RANK, RANK), place).astype(BF16)
            moved = moved.reshape(FAR_LEAF, RANK, 2 * RANK)
            leafw[t, :, pl.ds(0, RANK)] = moved
            leafw[t, :, pl.ds(RANK, RANK)] = moved

    for i in (0, 1, 2):
        loads[i].wait()
    upward((vals00, vals01), coefs0, boxes0)
    pl.semaphore_wait(barrier, len(greet))
    for i in (8, 9, 10, 11):
        loads[i].wait()
    targets = [lax.rem(pairs[0, n], GROUP) for n in range(SLOTS)]
    sources = [lax.rem(pairs[1, n], GROUP) for n in range(SLOTS)]


    pending = []

    class Sends:
        def __init__(self, p, k, whole):
            self.p, self.k = p, k
            pending.append((whole, send_sem.at[p, k]))

        def start(self, src, dst, peer, arrival=None):
            pltpu.make_async_remote_copy(
                src_ref=src, dst_ref=dst,
                send_sem=send_sem.at[self.p, self.k],
                recv_sem=recv_sem.at[self.p, self.k if arrival is None else arrival],
                device_id=peer, device_id_type=MESH,
            ).start()

    def finish(p, k, whole):
        pltpu.make_async_copy(whole, whole, recv_sem.at[p, k]).wait()

    V0, V1, C, YN, YF, Z1, Z2, Z3, Z4, X, K, R0, R1, W, S = range(15)
    z_chunks = ((Z1, 1, 3), (Z2, 3, 5), (Z3, 5, 7), (Z4, 7, 8))
    z_sem = {slot: k for k, a, b in z_chunks for slot in range(a, b)}

    for p in range(2):
        val, coef, box = (
            ((vals00, vals01), coefs0, boxes0),
            ((vals10, vals11), coefs1, boxes1),
        )[p]
        part, got = ((part0, got0), (part1, got1))[p]
        give, take = ((give0, take0), (give1, take1))[p]

        def send_values(h):
            group = Sends(p, (V0, V1)[h], val[h].at[pl.ds(0, 7 * LEAVES)])
            for d in FAR_FIRST:
                group.start(val[h].at[own], val[h].at[own], y_peer(d))

        def near_half(h):
            finish(p, (V0, V1)[h], val[h].at[pl.ds(0, 7 * LEAVES)])
            for n in range(0, SLOTS, 2):
                ahead = [dot_nt(val[h][sources[n + i]], blocks[n + i]) for i in range(2)]
                back = [dot(val[h][targets[n + i]], blocks[n + i]) for i in range(2)]
                contrib[h, pl.ds(n * HALF, RHS)] = jnp.concatenate(ahead, 0).astype(BF16)
                contrib[h, pl.ds((SLOTS + n) * HALF, RHS)] = jnp.concatenate(back, 0).astype(BF16)
            total = dot(scatter[...], contrib[h]).astype(BF16)
            part[h] = total.reshape(NY, LEAVES * HALF, PANELS)
            group = Sends(p, (R0, R1)[h], got.at[h])
            for d in FAR_FIRST:
                group.start(part.at[h, lax.rem(y + d, NY)], got.at[h, d - 1], y_peer(d))

        if p == 1:
            upward(val, coef, box)
        along_y = Sends(p, YN, box.at[pl.ds(1, 7)])
        for d in FAR_FIRST:
            slot = ORDER[8 - d]
            along_y.start(box.at[0], box.at[slot], y_peer(d), YN if slot < NEAR else YF)
        send_values(0)
        send_values(1)
        if p == 0:
            Sends(0, S, other_src).start(box_src_hbm, other_src, other)
        group = Sends(p, C, coef.at[pl.ds(0, 7)])
        for d in FAR_FIRST:
            group.start(coef.at[y], coef.at[y], y_peer(d))

        if p == 0:
            prepare()
            for i in (5, 6, 7):
                loads[i].wait()
            Sends(0, W, boxw.at[1]).start(boxw.at[0], boxw.at[1], other)
            finish(0, S, other_src)
            to_smem = pltpu.make_async_copy(other_src, other_src_smem, load_sem.at[8])
            to_smem.start()
            to_smem.wait()
            for g, src in enumerate((box_src, other_src_smem)):
                for j in range(FAR_BOX):
                    b = src[0, j]
                    by = lax.rem(lax.rem(b, NY) + NY - y, NY)
                    bx = lax.rem(lax.rem(lax.div(b, 2 * NY), NX) + NX - x, NX)
                    bz = lax.rem(lax.rem(lax.div(b, 2 * NY * NX), NZ) + NZ - z, NZ)
                    spot = bx * PLANE + ring_slot(bz) * NY + ring_slot(by)
                    held = lax.rem(lax.div(b, NY), 2) == core
                    where[g, j] = jnp.where(held, spot, BOXES)

        for k, a, b in ((YN, 0, NEAR), (YF, NEAR, ALL)):
            finish(p, k, box.at[pl.ds(max(a, 1), b - max(a, 1))])
            along_z = Sends(p, (Z1, Z2)[a > 0], box.at[pl.ds(0, 7 * (b - a))])
            for d in NEAR_FIRST:
                slot = ORDER[8 - d]
                along_z.start(
                    box.at[pl.ds(a, b - a)], box.at[pl.ds(8 * slot + a, b - a)],
                    z_peer(d), z_sem[slot],
                )

        along_x = Sends(p, X, box.at[pl.ds(PLANE, 3 * PLANE)])

        def send_x(a, b):
            for d in (2, 1, 3):
                along_x.start(
                    box.at[pl.ds(8 * a, 8 * (b - a))],
                    box.at[pl.ds((NX - d) * PLANE + 8 * a, 8 * (b - a))],
                    x_peer(d),
                )

        def forward(chunk):
            k, a, b = z_chunks[chunk]
            finish(p, k, box.at[pl.ds(8 * a, 8 * (b - a))])
            send_x(a, b)

        send_x(0, 1)
        near_half(0)
        for chunk in range(4):
            forward(chunk)
        near_half(1)

        finish(p, C, coef.at[pl.ds(0, 7)])
        for t in range(LEAVES):
            for j in range(FAR_LEAF):
                leaf = lax.rem(leaf_src[t, j], GROUP)
                tile = coef[lax.div(leaf, LEAVES), lax.div(lax.rem(leaf, LEAVES), 2)]
                keep = lax.shift_right_logical(lane, 6) == lax.rem(leaf, 2)
                leaflhs[t, :, pl.ds(j * 2 * RANK, 2 * RANK)] = jnp.where(
                    keep, tile.astype(F32), 0.0
                ).astype(BF16)
        pair = FAR_LEAF * 2 * RANK
        fields = []
        for t in range(LEAVES):
            fields.append(dot(leaflhs[t], leafw[t].reshape(pair, 2 * RANK)))
        leaf_field = jnp.concatenate([fields[0] + fields[1], fields[2] + fields[3]], axis=1)

        spread = jnp.concatenate(
            [leaf_field[:HALF]] * LEAVES + [leaf_field[HALF:]] * LEAVES, axis=0
        )
        spread = jnp.where(diagonal, spread, 0.0).astype(BF16)
        from_leaves = dot(spread, basis[...].reshape(WIDE, PANELS))

        finish(p, X, box.at[pl.ds(PLANE, 3 * PLANE)])
        if p == 0:
            finish(0, W, boxw.at[1])

        def box_part(g):
            for j in range(FAR_BOX):
                tile = box[where[g, j]].astype(F32)
                boxlhs[g, :, pl.ds(j * 2 * RANK, 2 * RANK)] = jnp.concatenate(
                    [jnp.where(low_half, tile, 0.0), jnp.where(low_half, 0.0, tile)], axis=0
                ).astype(BF16)
            return dot(boxlhs[g], boxw[g].reshape(FAR_BOX * 2 * RANK, RANK))

        give[...] = box_part(1)
        Sends(p, K, take).start(give, take, other)
        box_field = box_part(0)
        finish(p, K, take)
        box_field = (box_field + take[...]).astype(BF16)
        from_box = dot(box_field, down[...])

        result = []
        for h in range(2):
            finish(p, (R0, R1)[h], got.at[h])
            near = part[h, y].astype(F32)
            for d in range(1, NY):
                near = near + got[h, d - 1].astype(F32)
            near = near + from_leaves[h * LEAVES * HALF : (h + 1) * LEAVES * HALF]
            near = near + jnp.concatenate(
                [
                    from_box[h * HALF : (h + 1) * HALF, t * PANELS : (t + 1) * PANELS]
                    for t in range(LEAVES)
                ],
                axis=0,
            )
            near = near.astype(BF16).reshape(LEAVES, HALF, PANELS)
            if p == 0:
                (vals10, vals11)[h][own] = near
            else:
                last[h] = near
        for h in range(2):
            pltpu.make_async_copy(
                (vals10, vals11)[h].at[own] if p == 0 else last.at[h],
                out_hbm.at[p, :, pl.ds(h * HALF, HALF)],
                store_sem.at[p, h],
            ).start()

    for whole, sem in pending:
        pltpu.make_async_copy(whole, whole, sem).wait()
    for p in range(2):
        for h in range(2):
            pltpu.make_async_copy(
                (vals10, vals11)[h].at[own] if p == 0 else last.at[h],
                out_hbm.at[p, :, pl.ds(h * HALF, HALF)],
                store_sem.at[p, h],
            ).wait()


def on_device(
    panels, leaf_basis, transfer, leaf_sources, leaf_coupling,
    box_sources, box_coupling, near_blocks, near_pairs, near_count,
):
    hbm = pl.BlockSpec(memory_space=pl.ANY)
    products = jax.ShapeDtypeStruct((2, LEAVES, RHS, PANELS), BF16)
    values = pltpu.VMEM((GROUP, HALF, PANELS), BF16)
    coefs = pltpu.VMEM((NY, 2, RHS, 2 * RANK), BF16)
    boxes = pltpu.VMEM((BOXES + 1, HALF, 2 * RANK), BF16)
    part = pltpu.VMEM((2, NY, LEAVES * HALF, PANELS), BF16)
    got = pltpu.VMEM((2, NY - 1, LEAVES * HALF, PANELS), BF16)
    field = pltpu.VMEM((RHS, RANK), F32)
    both = pl.pallas_call(
        kernel,
        out_shape=products,
        in_specs=[hbm] * 10,
        out_specs=hbm,
        scratch_shapes=[
            pltpu.VMEM((LEAVES, RANK, PANELS), BF16),
            pltpu.VMEM((LEAVES, RANK, RANK), BF16),
            pltpu.VMEM((LEAVES, FAR_LEAF, RANK, RANK), BF16),
            pltpu.VMEM((2, FAR_BOX, 2 * RANK, RANK), BF16),
            pltpu.VMEM((SLOTS, PANELS, PANELS), BF16),
            pltpu.VMEM((WIDE, 2 * RANK), BF16),
            pltpu.VMEM((LEAVES, FAR_LEAF, 2 * RANK, 2 * RANK), BF16),
            pltpu.VMEM((GROUP * HALF, 2 * SLOTS * HALF), BF16),
            pltpu.VMEM((2, 2 * SLOTS * HALF, PANELS), BF16),
            values, values, values, values, coefs, coefs, boxes, boxes, part, part, got, got,
            pltpu.VMEM((2, LEAVES, HALF, PANELS), BF16),
            pltpu.VMEM((2, RHS, FAR_BOX * 2 * RANK), BF16),
            pltpu.VMEM((LEAVES, RHS, FAR_LEAF * 2 * RANK), BF16),
            field, field, field, field,
            pltpu.VMEM((1, FAR_BOX), jnp.int32),
            pltpu.SMEM((1, FAR_BOX), jnp.int32),
            pltpu.SMEM((2, SLOTS), jnp.int32),
            pltpu.SMEM((1,), jnp.int32),
            pltpu.SMEM((LEAVES, FAR_LEAF), jnp.int32),
            pltpu.SMEM((1, FAR_BOX), jnp.int32),
            pltpu.SMEM((2, FAR_BOX), jnp.int32),
            pltpu.VMEM((RANK, LEAVES * PANELS), BF16),
            pltpu.SemaphoreType.DMA((13,)),
            pltpu.SemaphoreType.DMA((2, 2)),
            pltpu.SemaphoreType.DMA((2, 15)),
            pltpu.SemaphoreType.DMA((2, 15)),
        ],
        compiler_params=pltpu.CompilerParams(
            collective_id=0, has_side_effects=True, vmem_limit_bytes=63 << 20
        ),
        name="two_products",
    )(
        near_pairs.T, near_count, leaf_sources, box_sources,
        panels, jnp.swapaxes(leaf_basis, 1, 2), transfer, leaf_coupling,
        box_coupling, near_blocks,
    )
    return both[0], both[1]


def solution(mesh):
    split = ("clus", "nbr")
    placed = (
        P(split, None, None),
        P(split, None, None),
        P(split, None, None),
        P(split, None),
        P(split, None, None, None),
        P(split, None),
        P(split, None, None, None),
        P(split, None, None),
        P(split, None),
        P(split),
    )
    return jax.shard_map(
        on_device,
        mesh=mesh,
        in_specs=placed,
        out_specs=(P(split, None, None), P(split, None, None)),
        check_vma=False,
    )
```

```python
import jax
import jax.numpy as jnp
from jax import lax
from jax.experimental import pallas as pl
from jax.experimental.pallas import tpu as pltpu
from jax.sharding import PartitionSpec as P

MESH = pl.DeviceIdType.LOGICAL
F32 = jnp.float32
BF16 = jnp.bfloat16
NY, NZ, NX = 8, 8, 4
LEAVES, RHS, PANELS, RANK = 4, 16, 256, 64
HALF = RHS // 2
WIDE = LEAVES * RANK
SLOTS, FAR_LEAF, FAR_BOX = 16, 8, 32
GROUP = NY * LEAVES
PLANE = NZ * NY
BOXES = NX * PLANE
NT = (((1,), (1,)), ((), ()))
FAR_FIRST = (4, 3, 5, 2, 6, 1, 7)
NEAR_FIRST = FAR_FIRST[::-1]
ORDER = {0: 0, 1: 1, 7: 2, 2: 3, 6: 4, 3: 5, 5: 6, 4: 7}
NEAR, ALL = 5, 8


def dot(a, b):
    return jnp.dot(a, b, preferred_element_type=F32)


def dot_nt(a, b):
    return lax.dot_general(a, b, NT, preferred_element_type=F32)


def iota(shape, dim):
    return lax.broadcasted_iota(jnp.int32, shape, dim)


def ring_slot(distance):
    return jnp.where(distance > 4, 2 * (8 - distance), jnp.maximum(2 * distance - 1, 0))


def kernel(
    pairs_hbm, count_hbm, leaf_src_hbm, box_src_hbm,
    panels_hbm, basis_hbm, transfer_hbm, leafc_hbm, boxc_hbm, blocks_hbm,
    out_hbm,
    basis, transfer, leafc, boxw, blocks, twice, leafw, scatter, contrib,
    vals00, vals01, vals10, vals11, coefs0, coefs1, boxes0, boxes1, part0, part1, got0, got1,
    last, boxlhs, leaflhs, give0, give1, take0, take1, other_src, other_src_smem,
    pairs, count, leaf_src, box_src, where, down, load_sem, store_sem, send_sem, recv_sem,
):
    clus = lax.axis_index("clus")
    y = lax.axis_index("nbr")
    core = lax.rem(clus, 2)
    x = lax.rem(lax.div(clus, 2), NX)
    z = lax.div(clus, 2 * NX)

    def at(zz, xx, cc, yy):
        return ((zz * NX + xx) * 2 + cc) * NY + yy

    def y_peer(d):
        return at(z, x, core, lax.rem(y + d, NY))

    def z_peer(d):
        return at(lax.rem(z + d, NZ), x, core, y)

    def x_peer(d):
        return at(z, lax.rem(x + d, NX), core, y)

    other = at(z, x, 1 - core, y)
    own = pl.ds(y * LEAVES, LEAVES)

    def load(i, src, dst):
        copy = pltpu.make_async_copy(src, dst, load_sem.at[i])
        copy.start()
        return copy

    loads = [
        load(0, panels_hbm.at[:, pl.ds(0, HALF)], vals00.at[own]),
        load(1, panels_hbm.at[:, pl.ds(HALF, HALF)], vals01.at[own]),
        load(2, basis_hbm, basis),
        load(3, transfer_hbm, transfer),
        load(4, leafc_hbm, leafc),
        load(5, boxc_hbm.at[0], boxw.at[0, :, pl.ds(0, RANK)]),
        load(6, boxc_hbm.at[0], boxw.at[0, :, pl.ds(RANK, RANK)]),
        load(7, blocks_hbm, blocks),
        load(9, pairs_hbm, pairs),
        load(10, count_hbm, count),
        load(11, leaf_src_hbm, leaf_src),
        load(12, box_src_hbm, box_src),
    ]

    barrier = pltpu.get_barrier_semaphore()
    greet = [y_peer(d) for d in FAR_FIRST] + [z_peer(d) for d in FAR_FIRST]
    greet += [x_peer(d) for d in (2, 1, 3)] + [other]
    for peer in greet:
        pl.semaphore_signal(barrier, inc=1, device_id=peer, device_id_type=MESH)

    lane = iota((1, 2 * RANK), 1)
    low_half = lane < RANK
    eye_row = iota((RANK, 2 * RANK), 0)
    eye_lane = iota((RANK, 2 * RANK), 1)
    diag_row = jnp.bitwise_and(lax.shift_right_logical(iota((LEAVES * RHS, WIDE), 0), 3), LEAVES - 1)
    diagonal = diag_row == lax.shift_right_logical(iota((LEAVES * RHS, WIDE), 1), 6)

    loads[3].wait()
    both = (jnp.bitwise_and(eye_lane, RANK - 1) == eye_row).astype(BF16)
    twice[...] = dot(transfer[...].reshape(WIDE, RANK), both).astype(BF16)

    def upward(val, coef, box):
        mine = jnp.concatenate(
            [val[h][own].reshape(LEAVES * HALF, PANELS) for h in range(2)], axis=0
        )
        every = dot_nt(mine, basis[...].reshape(WIDE, PANELS))
        every = jnp.where(diagonal, every, 0.0).reshape(2, LEAVES, HALF, WIDE)
        packed = jnp.sum(every, axis=1).reshape(RHS, WIDE).astype(BF16)
        coef[y, 0] = packed[:, : 2 * RANK]
        coef[y, 1] = packed[:, 2 * RANK :]
        wide = dot(packed, twice[...])
        box[0] = jnp.where(low_half, wide[:HALF], wide[HALF:]).astype(BF16)
        box[BOXES] = jnp.zeros((HALF, 2 * RANK), BF16)

    def prepare():
        side = iota((1, 2 * SLOTS * HALF), 1)
        slot = lax.shift_right_logical(side, 3)
        onto = jnp.full(side.shape, -1, jnp.int32)
        live_count = count[0]
        for n in range(SLOTS):
            live = n < live_count
            onto = jnp.where(slot == n, jnp.where(live, targets[n], -1), onto)
            apart = jnp.logical_and(live, targets[n] != sources[n])
            onto = jnp.where(slot == n + SLOTS, jnp.where(apart, sources[n], -1), onto)
        square = (GROUP * HALF, 2 * SLOTS * HALF)
        row = iota(square, 0)
        same = jnp.bitwise_and(row, HALF - 1) == jnp.bitwise_and(iota(square, 1), HALF - 1)
        hit = jnp.logical_and(same, lax.shift_right_logical(row, 3) == onto)
        scatter[...] = hit.astype(BF16)
        for t in range(LEAVES):
            down[:, pl.ds(t * PANELS, PANELS)] = lax.dot_general(
                transfer[t], basis[t], (((0,), (0,)), ((), ())), preferred_element_type=F32
            ).astype(BF16)
        loads[4].wait()
        for t in range(LEAVES):
            place = (eye_lane == eye_row + (t % 2) * RANK).astype(BF16)
            moved = dot(leafc[t].reshape(FAR_LEAF * RANK, RANK), place).astype(BF16)
            moved = moved.reshape(FAR_LEAF, RANK, 2 * RANK)
            leafw[t, :, pl.ds(0, RANK)] = moved
            leafw[t, :, pl.ds(RANK, RANK)] = moved

    for i in (0, 1, 2):
        loads[i].wait()
    upward((vals00, vals01), coefs0, boxes0)
    pl.semaphore_wait(barrier, len(greet))
    for i in (8, 9, 10, 11):
        loads[i].wait()
    targets = [lax.rem(pairs[0, n], GROUP) for n in range(SLOTS)]
    sources = [lax.rem(pairs[1, n], GROUP) for n in range(SLOTS)]


    pending = []

    class Sends:
        def __init__(self, p, k, whole):
            self.p, self.k = p, k
            pending.append((whole, send_sem.at[p, k]))

        def start(self, src, dst, peer, arrival=None):
            pltpu.make_async_remote_copy(
                src_ref=src, dst_ref=dst,
                send_sem=send_sem.at[self.p, self.k],
                recv_sem=recv_sem.at[self.p, self.k if arrival is None else arrival],
                device_id=peer, device_id_type=MESH,
            ).start()

    def finish(p, k, whole):
        pltpu.make_async_copy(whole, whole, recv_sem.at[p, k]).wait()

    V0, V1, C, YN, YF, X, K, R0, R1, W, S, Z1, Z2 = range(13)
    z_chunks = tuple((Z1 + i, i + 1, i + 2) for i in range(7))
    z_sem = {slot: k for k, a, b in z_chunks for slot in range(a, b)}

    def store(p, h):
        return pltpu.make_async_copy(
            (vals10, vals11)[h].at[own] if p == 0 else last.at[h],
            out_hbm.at[p, :, pl.ds(h * HALF, HALF)],
            store_sem.at[p, h],
        )

    for p in range(2):
        val, coef, box = (
            ((vals00, vals01), coefs0, boxes0),
            ((vals10, vals11), coefs1, boxes1),
        )[p]
        part, got = ((part0, got0), (part1, got1))[p]
        give, take = ((give0, take0), (give1, take1))[p]

        def send_values(h):
            group = Sends(p, (V0, V1)[h], val[h].at[pl.ds(0, 7 * LEAVES)])
            for d in FAR_FIRST:
                group.start(val[h].at[own], val[h].at[own], y_peer(d))

        def near_half(h):
            finish(p, (V0, V1)[h], val[h].at[pl.ds(0, 7 * LEAVES)])
            for n in range(0, SLOTS, 2):
                ahead = [dot_nt(val[h][sources[n + i]], blocks[n + i]) for i in range(2)]
                back = [dot(val[h][targets[n + i]], blocks[n + i]) for i in range(2)]
                contrib[h, pl.ds(n * HALF, RHS)] = jnp.concatenate(ahead, 0).astype(BF16)
                contrib[h, pl.ds((SLOTS + n) * HALF, RHS)] = jnp.concatenate(back, 0).astype(BF16)
            total = dot(scatter[...], contrib[h]).astype(BF16)
            part[h] = total.reshape(NY, LEAVES * HALF, PANELS)
            group = Sends(p, (R0, R1)[h], got.at[h])
            for d in FAR_FIRST:
                group.start(part.at[h, lax.rem(y + d, NY)], got.at[h, d - 1], y_peer(d))

        if p == 1:
            upward(val, coef, box)
        along_y = Sends(p, YN, box.at[pl.ds(1, 7)])
        for d in FAR_FIRST:
            slot = ORDER[8 - d]
            along_y.start(box.at[0], box.at[slot], y_peer(d), YN if slot < NEAR else YF)
        send_values(0)
        send_values(1)
        if p == 0:
            Sends(0, S, other_src).start(box_src_hbm, other_src, other)
        group = Sends(p, C, coef.at[pl.ds(0, 7)])
        for d in FAR_FIRST:
            group.start(coef.at[y], coef.at[y], y_peer(d))

        if p == 1:
            for h in range(2):
                store(0, h).start()
        if p == 0:
            prepare()
            for i in (5, 6, 7):
                loads[i].wait()
            Sends(0, W, boxw.at[1]).start(boxw.at[0], boxw.at[1], other)
            finish(0, S, other_src)
            to_smem = pltpu.make_async_copy(other_src, other_src_smem, load_sem.at[8])
            to_smem.start()
            to_smem.wait()
            for g, src in enumerate((box_src, other_src_smem)):
                for j in range(FAR_BOX):
                    b = src[0, j]
                    by = lax.rem(lax.rem(b, NY) + NY - y, NY)
                    bx = lax.rem(lax.rem(lax.div(b, 2 * NY), NX) + NX - x, NX)
                    bz = lax.rem(lax.rem(lax.div(b, 2 * NY * NX), NZ) + NZ - z, NZ)
                    spot = bx * PLANE + ring_slot(bz) * NY + ring_slot(by)
                    held = lax.rem(lax.div(b, NY), 2) == core
                    where[g, j] = jnp.where(held, spot, BOXES)

        for k, a, b in ((YN, 0, NEAR), (YF, NEAR, ALL)):
            finish(p, k, box.at[pl.ds(max(a, 1), b - max(a, 1))])
            along_z = Sends(p, (Z1, Z2)[a > 0], box.at[pl.ds(0, 7 * (b - a))])
            for d in NEAR_FIRST:
                slot = ORDER[8 - d]
                along_z.start(
                    box.at[pl.ds(a, b - a)], box.at[pl.ds(8 * slot + a, b - a)],
                    z_peer(d), z_sem[slot],
                )

        along_x = Sends(p, X, box.at[pl.ds(PLANE, 3 * PLANE)])

        def send_x(a, b):
            for d in (2, 1, 3):
                along_x.start(
                    box.at[pl.ds(8 * a, 8 * (b - a))],
                    box.at[pl.ds((NX - d) * PLANE + 8 * a, 8 * (b - a))],
                    x_peer(d),
                )

        def forward(chunk):
            k, a, b = z_chunks[chunk]
            finish(p, k, box.at[pl.ds(8 * a, 8 * (b - a))])
            send_x(a, b)

        send_x(0, 1)
        near_half(0)
        for chunk in range(7):
            forward(chunk)
        near_half(1)

        finish(p, C, coef.at[pl.ds(0, 7)])
        for t in range(LEAVES):
            for j in range(FAR_LEAF):
                leaf = lax.rem(leaf_src[t, j], GROUP)
                tile = coef[lax.div(leaf, LEAVES), lax.div(lax.rem(leaf, LEAVES), 2)]
                keep = lax.shift_right_logical(lane, 6) == lax.rem(leaf, 2)
                leaflhs[t, :, pl.ds(j * 2 * RANK, 2 * RANK)] = jnp.where(
                    keep, tile.astype(F32), 0.0
                ).astype(BF16)
        pair = FAR_LEAF * 2 * RANK
        fields = []
        for t in range(LEAVES):
            fields.append(dot(leaflhs[t], leafw[t].reshape(pair, 2 * RANK)))
        leaf_field = jnp.concatenate([fields[0] + fields[1], fields[2] + fields[3]], axis=1)

        spread = jnp.concatenate(
            [leaf_field[:HALF]] * LEAVES + [leaf_field[HALF:]] * LEAVES, axis=0
        )
        spread = jnp.where(diagonal, spread, 0.0).astype(BF16)
        from_leaves = dot(spread, basis[...].reshape(WIDE, PANELS))

        finish(p, X, box.at[pl.ds(PLANE, 3 * PLANE)])
        if p == 0:
            finish(0, W, boxw.at[1])

        def box_part(g):
            for j in range(FAR_BOX):
                tile = box[where[g, j]].astype(F32)
                boxlhs[g, :, pl.ds(j * 2 * RANK, 2 * RANK)] = jnp.concatenate(
                    [jnp.where(low_half, tile, 0.0), jnp.where(low_half, 0.0, tile)], axis=0
                ).astype(BF16)
            return dot(boxlhs[g], boxw[g].reshape(FAR_BOX * 2 * RANK, RANK))

        give[...] = box_part(1)
        Sends(p, K, take).start(give, take, other)
        box_field = box_part(0)
        totals = []
        for h in range(2):
            finish(p, (R0, R1)[h], got.at[h])
            near = part[h, y].astype(F32)
            for d in range(1, NY):
                near = near + got[h, d - 1].astype(F32)
            totals.append(near + from_leaves[h * LEAVES * HALF : (h + 1) * LEAVES * HALF])
        finish(p, K, take)
        box_field = (box_field + take[...]).astype(BF16)
        from_box = dot(box_field, down[...])
        for h in range(2):
            near = totals[h] + jnp.concatenate(
                [
                    from_box[h * HALF : (h + 1) * HALF, t * PANELS : (t + 1) * PANELS]
                    for t in range(LEAVES)
                ],
                axis=0,
            )
            near = near.astype(BF16).reshape(LEAVES, HALF, PANELS)
            if p == 0:
                (vals10, vals11)[h][own] = near
            else:
                last[h] = near

    for h in range(2):
        store(1, h).start()
    for whole, sem in pending:
        pltpu.make_async_copy(whole, whole, sem).wait()
    for p in range(2):
        for h in range(2):
            store(p, h).wait()


def on_device(
    panels, leaf_basis, transfer, leaf_sources, leaf_coupling,
    box_sources, box_coupling, near_blocks, near_pairs, near_count,
):
    hbm = pl.BlockSpec(memory_space=pl.ANY)
    products = jax.ShapeDtypeStruct((2, LEAVES, RHS, PANELS), BF16)
    values = pltpu.VMEM((GROUP, HALF, PANELS), BF16)
    coefs = pltpu.VMEM((NY, 2, RHS, 2 * RANK), BF16)
    boxes = pltpu.VMEM((BOXES + 1, HALF, 2 * RANK), BF16)
    part = pltpu.VMEM((2, NY, LEAVES * HALF, PANELS), BF16)
    got = pltpu.VMEM((2, NY - 1, LEAVES * HALF, PANELS), BF16)
    field = pltpu.VMEM((RHS, RANK), F32)
    both = pl.pallas_call(
        kernel,
        out_shape=products,
        in_specs=[hbm] * 10,
        out_specs=hbm,
        scratch_shapes=[
            pltpu.VMEM((LEAVES, RANK, PANELS), BF16),
            pltpu.VMEM((LEAVES, RANK, RANK), BF16),
            pltpu.VMEM((LEAVES, FAR_LEAF, RANK, RANK), BF16),
            pltpu.VMEM((2, FAR_BOX, 2 * RANK, RANK), BF16),
            pltpu.VMEM((SLOTS, PANELS, PANELS), BF16),
            pltpu.VMEM((WIDE, 2 * RANK), BF16),
            pltpu.VMEM((LEAVES, FAR_LEAF, 2 * RANK, 2 * RANK), BF16),
            pltpu.VMEM((GROUP * HALF, 2 * SLOTS * HALF), BF16),
            pltpu.VMEM((2, 2 * SLOTS * HALF, PANELS), BF16),
            values, values, values, values, coefs, coefs, boxes, boxes, part, part, got, got,
            pltpu.VMEM((2, LEAVES, HALF, PANELS), BF16),
            pltpu.VMEM((2, RHS, FAR_BOX * 2 * RANK), BF16),
            pltpu.VMEM((LEAVES, RHS, FAR_LEAF * 2 * RANK), BF16),
            field, field, field, field,
            pltpu.VMEM((1, FAR_BOX), jnp.int32),
            pltpu.SMEM((1, FAR_BOX), jnp.int32),
            pltpu.SMEM((2, SLOTS), jnp.int32),
            pltpu.SMEM((1,), jnp.int32),
            pltpu.SMEM((LEAVES, FAR_LEAF), jnp.int32),
            pltpu.SMEM((1, FAR_BOX), jnp.int32),
            pltpu.SMEM((2, FAR_BOX), jnp.int32),
            pltpu.VMEM((RANK, LEAVES * PANELS), BF16),
            pltpu.SemaphoreType.DMA((13,)),
            pltpu.SemaphoreType.DMA((2, 2)),
            pltpu.SemaphoreType.DMA((2, 18)),
            pltpu.SemaphoreType.DMA((2, 18)),
        ],
        compiler_params=pltpu.CompilerParams(
            collective_id=0, has_side_effects=True, vmem_limit_bytes=63 << 20
        ),
        name="two_products",
    )(
        near_pairs.T, near_count, leaf_sources, box_sources,
        panels, jnp.swapaxes(leaf_basis, 1, 2), transfer, leaf_coupling,
        box_coupling, near_blocks,
    )
    return both[0], both[1]


def solution(mesh):
    split = ("clus", "nbr")
    placed = (
        P(split, None, None),
        P(split, None, None),
        P(split, None, None),
        P(split, None),
        P(split, None, None, None),
        P(split, None),
        P(split, None, None, None),
        P(split, None, None),
        P(split, None),
        P(split),
    )
    return jax.shard_map(
        on_device,
        mesh=mesh,
        in_specs=placed,
        out_specs=(P(split, None, None), P(split, None, None)),
        check_vma=False,
    )
```
